32 devices in a mesh: pix: 4 (over y, core), chan: 8 (over z, x).
Axes of the slice: x: 2, y: 2, z: 4, core: 2. Of those that a mesh axis runs over, the one named last changes fastest.
Arguments:
- images: bfloat16 [2048, 32, 128], P('pix', 'chan'), may hold values from -6 to 6
- conv_weight: float32 [2048, 49], P('pix'), may hold values from -6 to 6
- conv_bias: float32 [2048], P('pix'), may hold values from -4 to 4
- norm_gain: float32 [2048], replicated, may hold values from 0.25 to 1.75
- norm_shift: float32 [2048], replicated, may hold values from -3 to 3
- up_weight: bfloat16 [2048, 8192], P(None, 'pix'), may hold values from -0.125 to 0.125
- up_bias: float32 [8192], P('pix'), may hold values from -3 to 3
- down_weight: bfloat16 [2048, 8192], P(None, 'pix'), may hold values from -0.09375 to 0.09375
- down_bias: float32 [2048], P('pix'), may hold values from -3 to 3
- layer_scale: float32 [2048], P('pix'), may hold values from 0.5 to 2
Outputs:
- block_out: bfloat16 [2048, 32, 128], P('pix', 'chan')
The draws below stay inside these ranges and needn't reach their ends.
All inputs are finite; a program needn't handle non-finite values.
Results may differ from the reference program's by a relative error of at most 0.006.
Values may be sent and summed in bfloat16 or wider, within the bound.
A program may use at most 64 MiB of HBM per device.

```python
import math
import jax
import jax.numpy as jnp
from jax import lax

C = 2048
F = 8192
W = 128
H = 32


def draw_conv_weight(key, part):
    key_base = jax.random.fold_in(key, 11)
    key_scale = jax.random.fold_in(key, 23)
    index = jnp.arange(C).astype(jnp.float32)
    rising = jnp.exp(math.log(3.0) * index / C)[:, None]
    spread = jnp.exp(jax.random.uniform(key_scale, (C, 1), jnp.float32, 0.0, math.log(3.5)))
    base = jnp.clip(jax.random.normal(key_base, (C, 49), jnp.float32), -4.0, 4.0)
    return base * rising * spread / 7.0


def spiked(array, own_key, source, target, blocks, factor):
    def block_of(position):
        return (jnp.arange(array.shape[position]) // (array.shape[position] // blocks)).reshape((-1,) + (1,) * (array.ndim - 1 - position))

    first = jax.random.permutation(own_key, blocks)[block_of(target)]
    second = (block_of(target) + blocks // 2) % blocks
    return jnp.where((block_of(source) == first) | (block_of(source) == second), factor * array, array)


def levels(rng, dims, split, low, largest):
    level = 1.0
    for position, parts in split:
        steps = jax.random.uniform(jax.random.fold_in(jax.random.fold_in(rng, 6), position), (parts,), jnp.float32, low / len(split), largest / len(split))
        level = level * jnp.repeat(jnp.exp(steps), dims[position] // parts).reshape((-1,) + (1,) * (len(dims) - 1 - position))
    return level


def normal_values(key, dims, scale, limit, shards=(), kind=jnp.bfloat16):
    entries = scale * jax.random.normal(key, dims, jnp.float32)
    if shards:
        entries = entries * levels(key, dims, shards, -0.22, 0.18)
    return jnp.clip(entries, -limit, limit).astype(kind)


def bell_draw_with(rng, extent, deviation, reach, cuts, heavy, dtype=jnp.bfloat16):
    values = deviation * jax.random.normal(rng, extent, jnp.float32)
    if cuts:
        values = values * levels(rng, extent, cuts, -0.22, 0.18)
    return jnp.clip(spiked(values, jax.random.fold_in(rng, 3), *heavy), -reach, reach).astype(dtype)


def setup_inputs(seed: int = 0) -> dict:
    keys = jax.random.split(jax.random.key(seed), 11)
    images = normal_values(keys[0], (C, H, W), 1.0, 6.0, ((0, 4), (1, 8)))
    conv_weight = draw_conv_weight(jax.random.fold_in(keys[10], 71), 0)
    conv_bias = normal_values(keys[2], (C,), 1.0, 4.0, ((0, 4),), jnp.float32)
    norm_gain = jnp.clip(1.0 + 0.15 * jax.random.normal(keys[3], (C,), jnp.float32), 0.25, 1.75)
    norm_shift = normal_values(keys[4], (C,), 0.5, 3.0, (), jnp.float32)
    up_weight = normal_values(keys[5], (C, F), C ** -0.5, 0.125, ((1, 4),))
    up_bias = normal_values(keys[6], (F,), 0.5, 3.0, ((0, 4),), jnp.float32)
    down_weight = bell_draw_with(keys[7], (C, F), F ** -0.5, 0.09375, ((1, 4),), (1, 0, 4, 2.0))
    down_bias = normal_values(keys[8], (C,), 0.5, 3.0, ((0, 4),), jnp.float32)
    layer_scale = jnp.clip(jnp.exp(math.log(2.0) - 1.3862944 * jax.random.uniform(keys[9], (C,), jnp.float32) ** levels(keys[9], (C,), ((0, 4),), -0.2, 0.2)), 0.5, 2.0)
    return {"images": images, "conv_weight": conv_weight, "conv_bias": conv_bias, "norm_gain": norm_gain, "norm_shift": norm_shift, "up_weight": up_weight, "up_bias": up_bias, "down_weight": down_weight, "down_bias": down_bias, "layer_scale": layer_scale}


def reference(images, conv_weight, conv_bias, norm_gain, norm_shift, up_weight, up_bias, down_weight, down_bias, layer_scale):
    chans, height, width = images.shape
    wide = jnp.pad(images.astype(jnp.float32), ((0, 0), (3, 3), (3, 3)))
    total = jnp.zeros((chans, height, width), jnp.float32)
    for first in range(7):
        for second in range(7):
            total = total + conv_weight[:, first * 7 + second][:, None, None] * wide[:, first:first + height, second:second + width]
    filtered = (total + conv_bias[:, None, None]).astype(jnp.bfloat16).reshape(chans, height * width)
    values = filtered.astype(jnp.float32)
    mean = lax.optimization_barrier(jnp.mean(values, axis=0))
    var = lax.optimization_barrier(jnp.mean(values * values, axis=0)) - mean * mean
    normed = ((values - mean) * jax.lax.rsqrt(var + 1e-06) * norm_gain[:, None] + norm_shift[:, None]).astype(jnp.bfloat16)
    pre = jnp.dot(up_weight.T, normed, preferred_element_type=jnp.float32)
    hidden = jax.nn.gelu(pre + up_bias[:, None], approximate=True).astype(jnp.bfloat16)
    mixed = jnp.dot(down_weight, hidden, preferred_element_type=jnp.float32)
    result = images.astype(jnp.float32).reshape(chans, height * width) + layer_scale[:, None] * (mixed + down_bias[:, None])
    return result.astype(jnp.bfloat16).reshape(chans, height, width)
```

```python
import functools

import jax
import jax.numpy as jnp
from jax import lax
from jax.experimental import pallas as pl
from jax.experimental.pallas import tpu as pltpu
from jax.sharding import PartitionSpec as P

MESH = pl.DeviceIdType.MESH
LANES = 128
TAPS = 7
HALO = 3
EDGE = 8
STRIP = 16


def kernel(
    n, m, x_ref, taps_ref, cbias_ref, gain_ref, shift_ref, ubias_ref, up_hbm, down_hbm, out_ref,
    up, down, near, far, wide, gath, normed, hidden, half_out, half_in, kept, cross_out, cross_in,
    up_sem, down_sem, near_send, near_recv, far_send, far_recv,
    gath_send, fwd_send, gath_recv, half_send, half_recv, cross_send, cross_recv,
):
    chunks, rows, width, _ = x_ref.shape
    pixels = rows * width
    chips = n // 2
    channels = n * chunks * LANES
    block = channels // n
    steps, sub = half_out.shape[0], half_out.shape[1]
    per_chip = steps // chips
    far_steps = steps - per_chip
    pix = lax.axis_index("pix")
    chan = lax.axis_index("chan")
    chip, core = pix // 2, pix % 2
    odd = chan % 2
    beside = chan + 1 - 2 * odd
    onward = chan + 2 - 4 * odd
    behind = chan - 2 + 4 * odd
    has_onward = (onward >= 0) & (onward < m)
    has_behind = (behind >= 0) & (behind < m)
    partner = pix + 1 - 2 * core

    def other(step):
        return ((chip + 1 + step) % chips) * 2 + core

    barrier = pltpu.get_barrier_semaphore()

    def greet(to_pix, to_chan):
        pl.semaphore_signal(
            barrier, inc=1, device_id={"pix": to_pix, "chan": to_chan}, device_id_type=MESH
        )

    greet(pix, beside)
    greet(partner, chan)
    for step in range(chips - 1):
        greet(other(step), chan)

    @pl.when(has_onward)
    def _():
        greet(pix, onward)

    @pl.when(has_behind)
    def _():
        greet(pix, behind)

    up_copy = pltpu.make_async_copy(up_hbm, up, up_sem)
    down_copy = pltpu.make_async_copy(down_hbm, down, down_sem)
    wide[...] = jnp.zeros_like(wide)

    @pl.when(jnp.logical_not(has_behind))
    def _():
        far[...] = jnp.zeros_like(far)

    pl.semaphore_wait(
        barrier, 1 + chips + has_onward.astype(jnp.int32) + has_behind.astype(jnp.int32)
    )

    def remote(src, dst, send, recv, to_pix, to_chan):
        return pltpu.make_async_remote_copy(
            src_ref=src, dst_ref=dst, send_sem=send, recv_sem=recv,
            device_id={"pix": to_pix, "chan": to_chan}, device_id_type=MESH,
        )

    def near_copy(k):
        return remote(x_ref.at[k], near.at[k], near_send.at[k], near_recv.at[k], pix, beside)

    def far_copy(k):
        return remote(
            near.at[k, pl.ds(1 - odd, HALO)], far.at[k], far_send.at[k], far_recv.at[k], pix, onward
        )

    def own_copy(k, step):
        slot = gath.at[pix * chunks + k]
        to = partner if step == chips - 1 else other(step)
        return remote(
            slot, slot, gath_send.at[step * chunks + k], gath_recv.at[pix * chunks + k], to, chan
        )

    def arrival(slot):
        return remote(gath.at[slot], gath.at[slot], up_sem, gath_recv.at[slot], partner, chan)

    def forward_copy(k, step):
        index = other(step) * chunks + k
        slot = gath.at[index]
        return remote(slot, slot, fwd_send.at[step * chunks + k], gath_recv.at[index], partner, chan)

    for k in range(chunks):
        near_copy(k).start()
    up_copy.start()
    down_copy.start()

    def pass_on(k):
        near_copy(k).wait_recv()

        @pl.when(has_onward)
        def _():
            far_copy(k).start()

    def filter_chunk(k):
        @pl.when(has_behind)
        def _():
            far_copy(k).wait_recv()

        inner = pl.ds(EDGE, width)
        wide[HALO : HALO + rows, inner, :] = x_ref[k].astype(jnp.float32)
        wide[pl.ds((HALO + rows) * (1 - odd), HALO), inner, :] = near[k, pl.ds(odd * (rows - HALO), HALO)].astype(
            jnp.float32
        )
        wide[pl.ds((HALO + rows) * odd, HALO), inner, :] = far[k].astype(jnp.float32)
        bias = cbias_ref[k]
        own = pix * chunks + k

        def strip(s, carry):
            first = pl.multiple_of(s * STRIP, STRIP)
            sums = [jnp.zeros((STRIP, LANES), jnp.float32) for _ in range(rows)]
            for b in range(TAPS):
                for i in range(rows + TAPS - 1):
                    piece = wide[i, pl.ds(first + (EDGE - HALO + b), STRIP), :]
                    for o in range(rows):
                        a = i - o
                        if 0 <= a < TAPS:
                            tap = a * TAPS + b
                            sums[o] = sums[o] + taps_ref[k, tap : tap + 1, :] * piece
            for o in range(rows):
                gath[own, pl.ds(pl.multiple_of(o * width + first, STRIP), STRIP), :] = (
                    sums[o] + bias
                ).astype(jnp.bfloat16)
            return carry

        lax.fori_loop(0, width // STRIP, strip, 0)
        for step in range(chips):
            own_copy(k, step).start()

    def relay(k):
        for step in range(chips - 1):
            arrival(other(step) * chunks + k).wait_recv()
            forward_copy(k, step).start()

    def front(k, carry):
        @pl.when(k < chunks)
        def _():
            pass_on(k)

        @pl.when((k >= 1) & (k < chunks + 1))
        def _():
            filter_chunk(k - 1)

        @pl.when(k >= 2)
        def _():
            relay(k - 2)

        return carry

    lax.fori_loop(0, chunks + 2, front, 0)

    def settle(k, carry):
        arrival(partner * chunks + k).wait_recv()
        for step in range(chips - 1):
            mate = other(step) + 1 - 2 * core
            arrival(mate * chunks + k).wait_recv()
        return carry

    lax.fori_loop(0, chunks, settle, 0)

    band = 64
    slots = n * chunks

    def normalise(s, carry):
        here = pl.ds(pl.multiple_of(s * band, band), band)
        first = jnp.zeros((band, LANES), jnp.float32)
        second = jnp.zeros((band, LANES), jnp.float32)
        for q in range(slots):
            v = gath[q, here, :].astype(jnp.float32)
            first = first + v
            second = second + v * v
        mean = jnp.sum(first, axis=1, keepdims=True) / channels
        var = jnp.sum(second, axis=1, keepdims=True) / channels - mean * mean
        scale = lax.rsqrt(var + 1e-06)
        for q in range(slots):
            lanes = slice(q * LANES, (q + 1) * LANES)
            v = gath[q, here, :].astype(jnp.float32)
            normed[here, lanes] = (
                (v - mean) * scale * gain_ref[:, lanes] + shift_ref[:, lanes]
            ).astype(jnp.bfloat16)
        return carry

    lax.fori_loop(0, pixels // band, normalise, 0)

    up_copy.wait()
    units = up.shape[1]
    tile = 256

    def expand(s, carry):
        cols = pl.ds(pl.multiple_of(s * tile, tile), tile)
        v = jnp.dot(normed[...], up[:, cols], preferred_element_type=jnp.float32) + ubias_ref[:, cols]
        hidden[:, cols] = (
            0.5 * v * (1.0 + jnp.tanh(0.7978845608 * (v + 0.044715 * (v * v * v))))
        ).astype(jnp.bfloat16)
        return carry

    lax.fori_loop(0, units // tile, expand, 0)

    down_copy.wait()

    def half_copy(t):
        return remote(half_out.at[t], half_in.at[t], half_send.at[t], half_recv.at[t], partner, chan)

    def cross_copy(t):
        return remote(
            cross_out.at[t], cross_in.at[t], cross_send.at[t], cross_recv.at[t],
            other(t // per_chip), chan,
        )

    def contract(start):
        part = down[pl.ds(pl.multiple_of(start, sub), sub), :]
        return lax.dot_general(
            part, hidden[...], (((1,), (1,)), ((), ())), preferred_element_type=jnp.float32
        )

    def combine(t):
        half_copy(t).wait_recv()

        @pl.when(t < far_steps)
        def _():
            cross_out[t] = (kept[t] + half_in[t].astype(jnp.float32)).astype(jnp.bfloat16)
            cross_copy(t).start()

        @pl.when(t >= far_steps)
        def _():
            kept[t] = kept[t] + half_in[t].astype(jnp.float32)

    def reduce(t, carry):
        @pl.when(t < steps)
        def _():
            owner = other(t // per_chip)
            away = owner + 1 - 2 * core
            row = (t % per_chip) * sub
            half_out[t] = contract(away * block + row).astype(jnp.bfloat16)
            half_copy(t).start()
            kept[t] = contract(owner * block + row)

        @pl.when(t >= 1)
        def _():
            combine(t - 1)

        return carry

    lax.fori_loop(0, steps + 1, reduce, 0)

    def finish(j, carry):
        total = kept[far_steps + j]
        for step in range(chips - 1):
            t = step * per_chip + j
            cross_copy(t).wait_recv()
            total = total + cross_in[t].astype(jnp.float32)
        out_ref[pl.ds(pl.multiple_of(j * sub, sub), sub), :] = total
        return carry

    lax.fori_loop(0, per_chip, finish, 0)

    for k in range(chunks):
        near_copy(k).wait_send()
        for step in range(chips):
            own_copy(k, step).wait_send()
        for step in range(chips - 1):
            forward_copy(k, step).wait_send()

    @pl.when(has_onward)
    def _():
        for k in range(chunks):
            far_copy(k).wait_send()

    for t in range(steps):
        half_copy(t).wait_send()
        if t < far_steps:
            cross_copy(t).wait_send()


def on_device(
    n, m,
    images, conv_weight, conv_bias, norm_gain, norm_shift, up_weight, up_bias, down_weight, down_bias,
    layer_scale,
):
    chans, rows, width = images.shape
    pixels = rows * width
    chunks = chans // LANES
    channels, units = up_weight.shape
    chips = n // 2
    sub = LANES
    steps = chips * (chans // sub)
    x = images.reshape(chunks, LANES, rows, width).transpose(0, 2, 3, 1)
    taps = conv_weight.reshape(chunks, LANES, TAPS * TAPS).transpose(0, 2, 1)
    vmem = pl.BlockSpec(memory_space=pltpu.VMEM)
    hbm = pl.BlockSpec(memory_space=pl.ANY)
    bf16, f32 = jnp.bfloat16, jnp.float32
    dma = pltpu.SemaphoreType.DMA
    mixed = pl.pallas_call(
        functools.partial(kernel, n, m),
        out_shape=jax.ShapeDtypeStruct((chans, pixels), f32),
        in_specs=[vmem] * 6 + [hbm] * 2,
        out_specs=vmem,
        scratch_shapes=[
            pltpu.VMEM((channels, units), bf16),
            pltpu.VMEM((channels, units), bf16),
            pltpu.VMEM((chunks, rows, width, LANES), bf16),
            pltpu.VMEM((chunks, HALO, width, LANES), bf16),
            pltpu.VMEM((rows + 2 * HALO, width + 2 * EDGE, LANES), f32),
            pltpu.VMEM((n * chunks, pixels, LANES), bf16),
            pltpu.VMEM((pixels, channels), bf16),
            pltpu.VMEM((pixels, units), bf16),
            pltpu.VMEM((steps, sub, pixels), bf16),
            pltpu.VMEM((steps, sub, pixels), bf16),
            pltpu.VMEM((steps, sub, pixels), f32),
            pltpu.VMEM((steps, sub, pixels), bf16),
            pltpu.VMEM((steps, sub, pixels), bf16),
            dma, dma,
            dma((chunks,)), dma((chunks,)), dma((chunks,)), dma((chunks,)),
            dma((chips * chunks,)), dma((chips * chunks,)), dma((n * chunks,)),
            dma((steps,)), dma((steps,)), dma((steps,)), dma((steps,)),
        ],
        compiler_params=pltpu.CompilerParams(collective_id=0, has_side_effects=True),
    )(
        x, taps, conv_bias.reshape(chunks, 1, LANES), norm_gain.reshape(1, channels),
        norm_shift.reshape(1, channels), up_bias.reshape(1, units), up_weight, down_weight,
    )
    result = images.astype(f32) + (
        layer_scale[:, None] * (mixed + down_bias[:, None])
    ).reshape(chans, rows, width)
    return result.astype(bf16)


def solution(mesh):
    placed = (
        P("pix", "chan", None),
        P("pix", None),
        P("pix"),
        P(),
        P(),
        P(None, "pix"),
        P("pix"),
        P(None, "pix"),
        P("pix"),
        P("pix"),
    )
    return jax.shard_map(
        functools.partial(on_device, mesh.shape["pix"], mesh.shape["chan"]),
        mesh=mesh, in_specs=placed, out_specs=P("pix", "chan", None), check_vma=False,
    )
```

```python
import functools

import jax
import jax.numpy as jnp
from jax import lax
from jax.experimental import pallas as pl
from jax.experimental.pallas import tpu as pltpu
from jax.sharding import PartitionSpec as P

MESH = pl.DeviceIdType.MESH
LANES = 128
TAPS = 7
HALO = 3
EDGE = 8
STRIP = 16
PARTS = 2


def kernel(
    n, m, x_ref, weight_ref, cbias_ref, gain_ref, shift_ref, ubias_ref, scale_ref, dbias_ref, up_hbm, down_hbm,
    out_ref,
    up, down, near, far, wide, square, taps, scales, biases, gath, normed, hidden,
    half_out, half_in, kept, cross_out, cross_in,
    up_sem, down_sem, near_send, near_recv, far_send, far_recv,
    gath_send, fwd_send, gath_recv, half_send, half_recv, cross_send, cross_recv,
):
    chunks, rows, width, _ = x_ref.shape
    span = width // PARTS
    pixels = rows * span
    chips = n // 2
    slots = n * chunks
    channels = slots * LANES
    block = channels // n
    sub = half_out.shape[1]
    steps = half_out.shape[0] // PARTS
    per_chip = steps // chips
    far_steps = steps - per_chip
    pix = lax.axis_index("pix")
    chan = lax.axis_index("chan")
    chip, core = pix // 2, pix % 2
    odd = chan % 2
    beside = chan + 1 - 2 * odd
    onward = chan + 2 - 4 * odd
    behind = chan - 2 + 4 * odd
    has_onward = (onward >= 0) & (onward < m)
    has_behind = (behind >= 0) & (behind < m)
    partner = pix + 1 - 2 * core

    def other(step):
        return ((chip + 1 + step) % chips) * 2 + core

    barrier = pltpu.get_barrier_semaphore()

    def greet(to_pix, to_chan):
        pl.semaphore_signal(
            barrier, inc=1, device_id={"pix": to_pix, "chan": to_chan}, device_id_type=MESH
        )

    greet(pix, beside)
    greet(partner, chan)
    for step in range(chips - 1):
        greet(other(step), chan)

    @pl.when(has_onward)
    def _():
        greet(pix, onward)

    @pl.when(has_behind)
    def _():
        greet(pix, behind)

    up_copy = pltpu.make_async_copy(up_hbm, up, up_sem)
    down_copy = pltpu.make_async_copy(down_hbm, down, down_sem)
    pl.semaphore_wait(
        barrier, 1 + chips + has_onward.astype(jnp.int32) + has_behind.astype(jnp.int32)
    )

    def remote(src, dst, send, recv, to_pix, to_chan):
        return pltpu.make_async_remote_copy(
            src_ref=src, dst_ref=dst, send_sem=send, recv_sem=recv,
            device_id={"pix": to_pix, "chan": to_chan}, device_id_type=MESH,
        )

    pieces = [(h, k) for h in range(PARTS) for k in range(chunks)]
    bounds = [0] + [span * (h + 1) + STRIP for h in range(PARTS - 1)] + [width]

    def fresh(h):
        return pl.ds(bounds[h], bounds[h + 1] - bounds[h])

    def near_copy(h, k):
        i = h * chunks + k
        return remote(
            x_ref.at[k, :, fresh(h)], near.at[k, :, fresh(h)], near_send.at[i], near_recv.at[i], pix, beside
        )

    def far_copy(h, k):
        i = h * chunks + k
        return remote(
            near.at[k, pl.ds(1 - odd, HALO), fresh(h)], far.at[k, :, fresh(h)],
            far_send.at[i], far_recv.at[i], pix, onward,
        )

    def own_copy(h, k, step):
        index = h * slots + pix * chunks + k
        to = partner if step == chips - 1 else other(step)
        return remote(
            gath.at[index], gath.at[index], gath_send.at[(step * PARTS + h) * chunks + k],
            gath_recv.at[index], to, chan,
        )

    def arrival(index):
        return remote(gath.at[index], gath.at[index], up_sem, gath_recv.at[index], partner, chan)

    def forward_copy(h, k, step):
        index = h * slots + other(step) * chunks + k
        return remote(
            gath.at[index], gath.at[index], fwd_send.at[(step * PARTS + h) * chunks + k],
            gath_recv.at[index], partner, chan,
        )

    for h, k in pieces:
        near_copy(h, k).start()
    up_copy.start()
    down_copy.start()

    wide[...] = jnp.zeros_like(wide)

    @pl.when(jnp.logical_not(has_behind))
    def _():
        far[...] = jnp.zeros_like(far)

    square[...] = jnp.zeros_like(square)
    for k in range(chunks):
        square[:, : TAPS * TAPS] = weight_ref[k * LANES : (k + 1) * LANES, :]
        taps[k] = square[...].T
    for j in range(per_chip):
        lanes = slice(j * sub, (j + 1) * sub)
        scales[j] = jnp.broadcast_to(scale_ref[:, lanes], (sub, sub)).T
        biases[j] = jnp.broadcast_to(dbias_ref[:, lanes], (sub, sub)).T

    def pass_on(h, k):
        near_copy(h, k).wait_recv()

        @pl.when(has_onward)
        def _():
            far_copy(h, k).start()

    def filter_piece(h, k):
        @pl.when(has_behind)
        def _():
            far_copy(h, k).wait_recv()

        low = max(span * h - STRIP, 0)
        high = bounds[h + 1]
        inner = slice(EDGE + low, EDGE + high)
        some = slice(low, high)
        wide[HALO : HALO + rows, inner, :] = x_ref[k, :, some].astype(jnp.float32)
        wide[pl.ds((HALO + rows) * (1 - odd), HALO), inner, :] = near[
            k, pl.ds(odd * (rows - HALO), HALO), some
        ].astype(jnp.float32)
        wide[pl.ds((HALO + rows) * odd, HALO), inner, :] = far[k, :, some].astype(jnp.float32)
        bias = cbias_ref[k]
        own = h * slots + pix * chunks + k

        def strip(s, carry):
            place = pl.multiple_of(s * STRIP, STRIP)
            sums = [jnp.zeros((STRIP, LANES), jnp.float32) for _ in range(rows)]
            for b in range(TAPS):
                for i in range(rows + TAPS - 1):
                    piece = wide[i, pl.ds(place + (span * h + EDGE - HALO + b), STRIP), :]
                    for o in range(rows):
                        a = i - o
                        if 0 <= a < TAPS:
                            tap = a * TAPS + b
                            sums[o] = sums[o] + taps[k, tap : tap + 1, :] * piece
            for o in range(rows):
                gath[own, pl.ds(pl.multiple_of(o * span + place, STRIP), STRIP), :] = (
                    sums[o] + bias
                ).astype(jnp.bfloat16)
            return carry

        lax.fori_loop(0, span // STRIP, strip, 0)
        for step in range(chips):
            own_copy(h, k, step).start()

    def relay(h, k):
        for step in range(chips - 1):
            arrival(h * slots + other(step) * chunks + k).wait_recv()
            forward_copy(h, k, step).start()

    def settle(h):
        def one(k, carry):
            arrival(h * slots + partner * chunks + k).wait_recv()
            for step in range(chips - 1):
                mate = other(step) + 1 - 2 * core
                arrival(h * slots + mate * chunks + k).wait_recv()
            return carry

        lax.fori_loop(0, chunks, one, 0)

    count = len(pieces)
    early = chunks
    lag = 3
    for i in range(count + 1):
        if i < count:
            pass_on(*pieces[i])
        if i >= 1:
            filter_piece(*pieces[i - 1])
        if i >= lag and i - lag < early:
            relay(*pieces[i - lag])
    for i in range(max(count + 1 - lag, 0), early):
        relay(*pieces[i])

    band = 64

    def normalise(h):
        def one(s, carry):
            here = pl.ds(pl.multiple_of(s * band, band), band)
            first = jnp.zeros((band, LANES), jnp.float32)
            second = jnp.zeros((band, LANES), jnp.float32)
            for q in range(slots):
                v = gath[h * slots + q, here, :].astype(jnp.float32)
                first = first + v
                second = second + v * v
            mean = jnp.sum(first, axis=1, keepdims=True) / channels
            var = jnp.sum(second, axis=1, keepdims=True) / channels - mean * mean
            scale = lax.rsqrt(var + 1e-06)
            for q in range(slots):
                lanes = slice(q * LANES, (q + 1) * LANES)
                v = gath[h * slots + q, here, :].astype(jnp.float32)
                normed[here, lanes] = (
                    (v - mean) * scale * gain_ref[:, lanes] + shift_ref[:, lanes]
                ).astype(jnp.bfloat16)
            return carry

        lax.fori_loop(0, pixels // band, one, 0)

    units = up.shape[1]
    tile = 256
    pair = 2

    def gelu(v):
        return 0.5 * v * (1.0 + jnp.tanh(0.7978845608 * (v + 0.044715 * (v * v * v))))

    def expand(h):
        def one(s, carry):
            if h + 1 < PARTS:
                @pl.when(s < chunks)
                def _():
                    relay(h + 1, s)

            cols = [
                pl.ds(pl.multiple_of(s * (pair * tile), pair * tile) + u * tile, tile) for u in range(pair)
            ]
            sums = [
                jnp.dot(normed[...], up[:, c], preferred_element_type=jnp.float32) + ubias_ref[:, c]
                for c in cols
            ]
            for c, v in zip(cols, sums):
                hidden[:, c] = gelu(v).astype(jnp.bfloat16)
            return carry

        rounds = units // (pair * tile)
        lax.fori_loop(0, rounds, one, 0)
        if h + 1 < PARTS:
            for k in range(rounds, chunks):
                relay(h + 1, k)

    def half_copy(h, t):
        i = h * steps + t
        return remote(half_out.at[i], half_in.at[i], half_send.at[i], half_recv.at[i], partner, chan)

    def cross_copy(h, t):
        i = h * steps + t
        return remote(
            cross_out.at[i], cross_in.at[i], cross_send.at[i], cross_recv.at[i],
            other(t // per_chip), chan,
        )

    def contract(start):
        part = down[pl.ds(pl.multiple_of(start, sub), sub), :]
        return lax.dot_general(
            part, hidden[...], (((1,), (1,)), ((), ())), preferred_element_type=jnp.float32
        )

    def combine(h, t):
        half_copy(h, t).wait_recv()
        i = h * steps + t

        @pl.when(t < far_steps)
        def _():
            cross_out[i] = (kept[i] + half_in[i].astype(jnp.float32)).astype(jnp.bfloat16)
            cross_copy(h, t).start()

        @pl.when(t >= far_steps)
        def _():
            kept[i] = kept[i] + half_in[i].astype(jnp.float32)

    def reduce(h):
        def one(t, carry):
            @pl.when(t < steps)
            def _():
                owner = other(t // per_chip)
                away = owner + 1 - 2 * core
                row = (t % per_chip) * sub
                half_out[h * steps + t] = contract(away * block + row).astype(jnp.bfloat16)
                half_copy(h, t).start()
                kept[h * steps + t] = contract(owner * block + row)

            @pl.when(t >= 1)
            def _():
                combine(h, t - 1)

            return carry

        lax.fori_loop(0, steps + 1, one, 0)

    for h in range(PARTS):
        settle(h)
        normalise(h)
        if h == 0:
            up_copy.wait()
        expand(h)
        if h == 0:
            down_copy.wait()
        reduce(h)

    def finish(j, carry):
        totals = []
        for h in range(PARTS):
            total = kept[h * steps + far_steps + j]
            for step in range(chips - 1):
                t = step * per_chip + j
                cross_copy(h, t).wait_recv()
                total = total + cross_in[h * steps + t].astype(jnp.float32)
            totals.append(total)
        here = pl.ds(pl.multiple_of(j * sub, sub), sub)
        for r in range(rows):
            line = jnp.concatenate([total[:, r * span : (r + 1) * span] for total in totals], axis=1)
            out_ref[here, r * width : (r + 1) * width] = scales[j] * (line + biases[j])
        return carry

    lax.fori_loop(0, per_chip, finish, 0)

    for h, k in pieces:
        near_copy(h, k).wait_send()
        for step in range(chips):
            own_copy(h, k, step).wait_send()
        for step in range(chips - 1):
            forward_copy(h, k, step).wait_send()

    @pl.when(has_onward)
    def _():
        for h, k in pieces:
            far_copy(h, k).wait_send()

    for h in range(PARTS):
        def sent(t, carry):
            half_copy(h, t).wait_send()

            @pl.when(t < far_steps)
            def _():
                cross_copy(h, t).wait_send()

            return carry

        lax.fori_loop(0, steps, sent, 0)


def on_device(
    n, m,
    images, conv_weight, conv_bias, norm_gain, norm_shift, up_weight, up_bias, down_weight, down_bias,
    layer_scale,
):
    chans, rows, width = images.shape
    pixels = rows * width
    chunks = chans // LANES
    channels, units = up_weight.shape
    chips = n // 2
    sub = LANES
    steps = chips * (chans // sub)
    x = images.reshape(chunks, LANES, rows, width).transpose(0, 2, 3, 1)
    span = width // PARTS
    part = rows * span
    vmem = pl.BlockSpec(memory_space=pltpu.VMEM)
    hbm = pl.BlockSpec(memory_space=pl.ANY)
    bf16, f32 = jnp.bfloat16, jnp.float32
    dma = pltpu.SemaphoreType.DMA
    mixed = pl.pallas_call(
        functools.partial(kernel, n, m),
        out_shape=jax.ShapeDtypeStruct((chans, pixels), f32),
        in_specs=[vmem] * 8 + [hbm] * 2,
        out_specs=vmem,
        scratch_shapes=[
            pltpu.VMEM((channels, units), bf16),
            pltpu.VMEM((channels, units), bf16),
            pltpu.VMEM((chunks, rows, width, LANES), bf16),
            pltpu.VMEM((chunks, HALO, width, LANES), bf16),
            pltpu.VMEM((rows + 2 * HALO, width + 2 * EDGE, LANES), f32),
            pltpu.VMEM((LANES, LANES), f32),
            pltpu.VMEM((chunks, LANES, LANES), f32),
            pltpu.VMEM((chans // sub, sub, sub), f32),
            pltpu.VMEM((chans // sub, sub, sub), f32),
            pltpu.VMEM((PARTS * n * chunks, part, LANES), bf16),
            pltpu.VMEM((part, channels), bf16),
            pltpu.VMEM((part, units), bf16),
            pltpu.VMEM((PARTS * steps, sub, part), bf16),
            pltpu.VMEM((PARTS * steps, sub, part), bf16),
            pltpu.VMEM((PARTS * steps, sub, part), f32),
            pltpu.VMEM((PARTS * steps, sub, part), bf16),
            pltpu.VMEM((PARTS * steps, sub, part), bf16),
            dma, dma,
            dma((PARTS * chunks,)), dma((PARTS * chunks,)), dma((PARTS * chunks,)), dma((PARTS * chunks,)),
            dma((PARTS * chips * chunks,)), dma((PARTS * chips * chunks,)), dma((PARTS * n * chunks,)),
            dma((PARTS * steps,)), dma((PARTS * steps,)), dma((PARTS * steps,)), dma((PARTS * steps,)),
        ],
        compiler_params=pltpu.CompilerParams(collective_id=0, has_side_effects=True),
    )(
        x, conv_weight, conv_bias.reshape(chunks, 1, LANES), norm_gain.reshape(1, channels),
        norm_shift.reshape(1, channels), up_bias.reshape(1, units), layer_scale.reshape(1, chans),
        down_bias.reshape(1, chans), up_weight, down_weight,
    )
    return (images.astype(f32) + mixed.reshape(chans, rows, width)).astype(bf16)


def solution(mesh):
    placed = (
        P("pix", "chan", None),
        P("pix", None),
        P("pix"),
        P(),
        P(),
        P(None, "pix"),
        P("pix"),
        P(None, "pix"),
        P("pix"),
        P("pix"),
    )
    return jax.shard_map(
        functools.partial(on_device, mesh.shape["pix"], mesh.shape["chan"]),
        mesh=mesh, in_specs=placed, out_specs=P("pix", "chan", None), check_vma=False,
    )
```

```python
import functools

import jax
import jax.numpy as jnp
from jax import lax
from jax.experimental import pallas as pl
from jax.experimental.pallas import tpu as pltpu
from jax.sharding import PartitionSpec as P

MESH = pl.DeviceIdType.MESH
LANES = 128
TAPS = 7
HALO = 3
EDGE = 8
STRIP = 16
PARTS = 1
GROUP = 2


def kernel(
    n, m, x_ref, weight_ref, cbias_ref, gain_ref, shift_ref, ubias_ref, scale_ref, dbias_ref, up_hbm, down_hbm,
    out_ref,
    up, down, near, far, wide, residual, scales, biases, gath, normed, hidden,
    half_out, half_in, kept, cross_out, cross_in,
    up_sem, down_sem, near_send, near_recv, far_send, far_recv,
    gath_send, fwd_send, gath_recv, half_send, half_recv, cross_send, cross_recv,
):
    chunks, rows, width, _ = x_ref.shape
    span = width // PARTS
    pixels = rows * span
    chips = n // 2
    slots = n * chunks
    channels = slots * LANES
    block = channels // n
    sub = half_out.shape[1]
    steps = half_out.shape[0] // PARTS
    per_chip = steps // chips
    far_steps = steps - per_chip
    pix = lax.axis_index("pix")
    chan = lax.axis_index("chan")
    chip, core = pix // 2, pix % 2
    odd = chan % 2
    beside = chan + 1 - 2 * odd
    onward = chan + 2 - 4 * odd
    behind = chan - 2 + 4 * odd
    has_onward = (onward >= 0) & (onward < m)
    has_behind = (behind >= 0) & (behind < m)
    partner = pix + 1 - 2 * core

    def other(step):
        return ((chip + 1 + step) % chips) * 2 + core

    barrier = pltpu.get_barrier_semaphore()

    def greet(to_pix, to_chan):
        pl.semaphore_signal(
            barrier, inc=1, device_id={"pix": to_pix, "chan": to_chan}, device_id_type=MESH
        )

    greet(pix, beside)
    greet(partner, chan)
    for step in range(chips - 1):
        greet(other(step), chan)

    @pl.when(has_onward)
    def _():
        greet(pix, onward)

    @pl.when(has_behind)
    def _():
        greet(pix, behind)

    up_copy = pltpu.make_async_copy(up_hbm, up, up_sem)
    down_copy = pltpu.make_async_copy(down_hbm, down, down_sem)
    pl.semaphore_wait(
        barrier, 1 + chips + has_onward.astype(jnp.int32) + has_behind.astype(jnp.int32)
    )

    def remote(src, dst, send, recv, to_pix, to_chan):
        return pltpu.make_async_remote_copy(
            src_ref=src, dst_ref=dst, send_sem=send, recv_sem=recv,
            device_id={"pix": to_pix, "chan": to_chan}, device_id_type=MESH,
        )

    pieces = [(h, k) for h in range(PARTS) for k in range(chunks)]
    bounds = [0] + [span * (h + 1) + STRIP for h in range(PARTS - 1)] + [width]

    def fresh(h):
        return pl.ds(bounds[h], bounds[h + 1] - bounds[h])

    def near_copy(h, k):
        i = h * chunks + k
        return remote(
            x_ref.at[k, :, fresh(h)], near.at[k, :, fresh(h)], near_send.at[i], near_recv.at[i], pix, beside
        )

    def far_copy(h, k):
        i = h * chunks + k
        return remote(
            near.at[k, pl.ds(1 - odd, HALO), fresh(h)], far.at[k, :, fresh(h)],
            far_send.at[i], far_recv.at[i], pix, onward,
        )

    def own_copy(h, k, step):
        index = h * slots + pix * chunks + k
        to = partner if step == chips - 1 else other(step)
        return remote(
            gath.at[index], gath.at[index], gath_send.at[(step * PARTS + h) * chunks + k],
            gath_recv.at[index], to, chan,
        )

    def arrival(index):
        return remote(gath.at[index], gath.at[index], up_sem, gath_recv.at[index], partner, chan)

    def forward_copy(h, k, step):
        index = h * slots + other(step) * chunks + k
        return remote(
            gath.at[index], gath.at[index], fwd_send.at[(step * PARTS + h) * chunks + k],
            gath_recv.at[index], partner, chan,
        )

    for h, k in pieces:
        near_copy(h, k).start()
    up_copy.start()
    down_copy.start()

    wide[...] = jnp.zeros_like(wide)

    @pl.when(jnp.logical_not(has_behind))
    def _():
        far[...] = jnp.zeros_like(far)

    for k in range(chunks):
        for row in range(rows):
            residual[k * LANES : (k + 1) * LANES, row * width : (row + 1) * width] = (
                x_ref[k, row].astype(jnp.float32).T
            )
    for j in range(per_chip):
        lanes = slice(j * sub, (j + 1) * sub)
        scales[j] = jnp.broadcast_to(scale_ref[:, lanes], (width, sub)).T
        biases[j] = jnp.broadcast_to(dbias_ref[:, lanes], (width, sub)).T

    def pass_on(h, k):
        near_copy(h, k).wait_recv()

        @pl.when(has_onward)
        def _():
            far_copy(h, k).start()

    def filter_piece(h, k):
        @pl.when(has_behind)
        def _():
            far_copy(h, k).wait_recv()

        low = max(span * h - STRIP, 0)
        high = bounds[h + 1]
        inner = slice(EDGE + low, EDGE + high)
        some = slice(low, high)
        wide[HALO : HALO + rows, inner, :] = x_ref[k, :, some].astype(jnp.float32)
        wide[pl.ds((HALO + rows) * (1 - odd), HALO), inner, :] = near[
            k, pl.ds(odd * (rows - HALO), HALO), some
        ].astype(jnp.float32)
        wide[pl.ds((HALO + rows) * odd, HALO), inner, :] = far[k, :, some].astype(jnp.float32)
        bias = cbias_ref[k]
        own = h * slots + pix * chunks + k

        def strip(s, carry):
            place = pl.multiple_of(s * STRIP, STRIP)
            sums = [jnp.zeros((STRIP, LANES), jnp.float32) for _ in range(rows)]
            for b in range(TAPS):
                for i in range(rows + TAPS - 1):
                    piece = wide[i, pl.ds(place + (span * h + EDGE - HALO + b), STRIP), :]
                    for o in range(rows):
                        a = i - o
                        if 0 <= a < TAPS:
                            tap = a * TAPS + b
                            sums[o] = sums[o] + weight_ref[tap : tap + 1, k * LANES : (k + 1) * LANES] * piece
            for o in range(rows):
                gath[own, pl.ds(pl.multiple_of(o * span + place, STRIP), STRIP), :] = (
                    sums[o] + bias
                ).astype(jnp.bfloat16)
            return carry

        lax.fori_loop(0, span // STRIP, strip, 0)
        for step in range(chips):
            own_copy(h, k, step).start()

    def relay(h, k):
        for step in range(chips - 1):
            arrival(h * slots + other(step) * chunks + k).wait_recv()
            forward_copy(h, k, step).start()

    def settle(h):
        def one(k, carry):
            arrival(h * slots + partner * chunks + k).wait_recv()
            for step in range(chips - 1):
                mate = other(step) + 1 - 2 * core
                arrival(h * slots + mate * chunks + k).wait_recv()
            return carry

        lax.fori_loop(0, chunks, one, 0)

    count = len(pieces)
    early = chunks
    lag = 3
    for i in range(count + 1):
        if i < count:
            pass_on(*pieces[i])
        if i >= 1:
            filter_piece(*pieces[i - 1])
        if i >= lag and i - lag < early:
            relay(*pieces[i - lag])
    for i in range(max(count + 1 - lag, 0), early):
        relay(*pieces[i])

    band = 64

    def normalise(h):
        def one(s, carry):
            here = pl.ds(pl.multiple_of(s * band, band), band)
            first = jnp.zeros((band, LANES), jnp.float32)
            second = jnp.zeros((band, LANES), jnp.float32)
            for q in range(slots):
                v = gath[h * slots + q, here, :].astype(jnp.float32)
                first = first + v
                second = second + v * v
            mean = jnp.sum(first, axis=1, keepdims=True) / channels
            var = jnp.sum(second, axis=1, keepdims=True) / channels - mean * mean
            scale = lax.rsqrt(var + 1e-06)
            for q in range(slots):
                lanes = slice(q * LANES, (q + 1) * LANES)
                v = gath[h * slots + q, here, :].astype(jnp.float32)
                normed[here, lanes] = (
                    (v - mean) * scale * gain_ref[:, lanes] + shift_ref[:, lanes]
                ).astype(jnp.bfloat16)
            return carry

        lax.fori_loop(0, pixels // band, one, 0)

    units = up.shape[1]
    tile = 256
    pair = 2

    def gelu(v):
        return 0.5 * v * (1.0 + jnp.tanh(0.7978845608 * (v + 0.044715 * (v * v * v))))

    def expand(h):
        def one(s, carry):
            if h + 1 < PARTS:
                @pl.when(s < chunks)
                def _():
                    relay(h + 1, s)

            cols = [
                pl.ds(pl.multiple_of(s * (pair * tile), pair * tile) + u * tile, tile) for u in range(pair)
            ]
            sums = [
                jnp.dot(normed[...], up[:, c], preferred_element_type=jnp.float32) + ubias_ref[:, c]
                for c in cols
            ]
            for c, v in zip(cols, sums):
                hidden[:, c] = gelu(v).astype(jnp.bfloat16)
            return carry

        rounds = units // (pair * tile)
        lax.fori_loop(0, rounds, one, 0)
        if h + 1 < PARTS:
            for k in range(rounds, chunks):
                relay(h + 1, k)

    def half_copy(h, t):
        i = h * steps + t
        return remote(half_out.at[i], half_in.at[i], half_send.at[i], half_recv.at[i], partner, chan)

    def cross_copy(h, t):
        i = h * steps + t
        return remote(
            cross_out.at[i], cross_in.at[i], cross_send.at[i], cross_recv.at[i],
            other(t // per_chip), chan,
        )

    def contract(start):
        part = down[pl.ds(pl.multiple_of(start, sub), sub), :]
        return lax.dot_general(
            part, hidden[...], (((1,), (1,)), ((), ())), preferred_element_type=jnp.float32
        )

    def combine(h, t):
        half_copy(h, t).wait_recv()
        i = h * steps + t

        @pl.when(t < far_steps)
        def _():
            cross_out[i] = (kept[i] + half_in[i].astype(jnp.float32)).astype(jnp.bfloat16)
            cross_copy(h, t).start()

        @pl.when(t >= far_steps)
        def _():
            kept[i] = kept[i] + half_in[i].astype(jnp.float32)

    def reduce(h):
        def one(t, carry):
            @pl.when(t < steps)
            def _():
                owner = other(t // per_chip)
                away = owner + 1 - 2 * core
                row = (t % per_chip) * sub
                half_out[h * steps + t] = contract(away * block + row).astype(jnp.bfloat16)
                half_copy(h, t).start()
                kept[h * steps + t] = contract(owner * block + row)

            @pl.when(t >= 1)
            def _():
                combine(h, t - 1)

            return carry

        lax.fori_loop(0, steps + 1, one, 0)

    for h in range(PARTS):
        settle(h)
        normalise(h)
        if h == 0:
            up_copy.wait()
        expand(h)
        if h == 0:
            down_copy.wait()
        reduce(h)

    def finish(j, carry):
        totals = []
        for h in range(PARTS):
            total = kept[h * steps + far_steps + j]
            for step in range(chips - 1):
                t = step * per_chip + j
                cross_copy(h, t).wait_recv()
                total = total + cross_in[h * steps + t].astype(jnp.float32)
            totals.append(total)
        here = pl.ds(pl.multiple_of(j * sub, sub), sub)
        for r in range(rows):
            line = jnp.concatenate([total[:, r * span : (r + 1) * span] for total in totals], axis=1)
            columns = slice(r * width, (r + 1) * width)
            out_ref[here, columns] = (
                residual[here, columns] + scales[j] * (line + biases[j])
            ).astype(out_ref.dtype)
        return carry

    lax.fori_loop(0, per_chip, finish, 0)

    for h, k in pieces:
        near_copy(h, k).wait_send()
        for step in range(chips):
            own_copy(h, k, step).wait_send()
        for step in range(chips - 1):
            forward_copy(h, k, step).wait_send()

    @pl.when(has_onward)
    def _():
        for h, k in pieces:
            far_copy(h, k).wait_send()

    for h in range(PARTS):
        def sent(t, carry):
            half_copy(h, t).wait_send()

            @pl.when(t < far_steps)
            def _():
                cross_copy(h, t).wait_send()

            return carry

        lax.fori_loop(0, steps, sent, 0)


def on_device(
    n, m,
    images, conv_weight, conv_bias, norm_gain, norm_shift, up_weight, up_bias, down_weight, down_bias,
    layer_scale,
):
    chans, rows, width = images.shape
    pixels = rows * width
    chunks = chans // LANES
    channels, units = up_weight.shape
    chips = n // 2
    sub = min(GROUP * LANES, chans)
    steps = chips * (chans // sub)
    x = images.reshape(chunks, LANES, rows, width).transpose(0, 2, 3, 1)
    span = width // PARTS
    part = rows * span
    vmem = pl.BlockSpec(memory_space=pltpu.VMEM)
    hbm = pl.BlockSpec(memory_space=pl.ANY)
    bf16, f32 = jnp.bfloat16, jnp.float32
    dma = pltpu.SemaphoreType.DMA
    result = pl.pallas_call(
        functools.partial(kernel, n, m),
        out_shape=jax.ShapeDtypeStruct((chans, pixels), bf16),
        in_specs=[vmem] * 8 + [hbm] * 2,
        out_specs=vmem,
        scratch_shapes=[
            pltpu.VMEM((channels, units), bf16),
            pltpu.VMEM((channels, units), bf16),
            pltpu.VMEM((chunks, rows, width, LANES), bf16),
            pltpu.VMEM((chunks, HALO, width, LANES), bf16),
            pltpu.VMEM((rows + 2 * HALO, width + 2 * EDGE, LANES), f32),
            pltpu.VMEM((chans, pixels), f32),
            pltpu.VMEM((chans // sub, sub, width), f32),
            pltpu.VMEM((chans // sub, sub, width), f32),
            pltpu.VMEM((PARTS * n * chunks, part, LANES), bf16),
            pltpu.VMEM((part, channels), bf16),
            pltpu.VMEM((part, units), bf16),
            pltpu.VMEM((PARTS * steps, sub, part), bf16),
            pltpu.VMEM((PARTS * steps, sub, part), bf16),
            pltpu.VMEM((PARTS * steps, sub, part), f32),
            pltpu.VMEM((PARTS * steps, sub, part), bf16),
            pltpu.VMEM((PARTS * steps, sub, part), bf16),
            dma, dma,
            dma((PARTS * chunks,)), dma((PARTS * chunks,)), dma((PARTS * chunks,)), dma((PARTS * chunks,)),
            dma((PARTS * chips * chunks,)), dma((PARTS * chips * chunks,)), dma((PARTS * n * chunks,)),
            dma((PARTS * steps,)), dma((PARTS * steps,)), dma((PARTS * steps,)), dma((PARTS * steps,)),
        ],
        compiler_params=pltpu.CompilerParams(collective_id=0, has_side_effects=True),
    )(
        x, conv_weight.T, conv_bias.reshape(chunks, 1, LANES), norm_gain.reshape(1, channels),
        norm_shift.reshape(1, channels), up_bias.reshape(1, units), layer_scale.reshape(1, chans),
        down_bias.reshape(1, chans), up_weight, down_weight,
    )
    return result.reshape(chans, rows, width)


def solution(mesh):
    placed = (
        P("pix", "chan", None),
        P("pix", None),
        P("pix"),
        P(),
        P(),
        P(None, "pix"),
        P("pix"),
        P(None, "pix"),
        P("pix"),
        P("pix"),
    )
    return jax.shard_map(
        functools.partial(on_device, mesh.shape["pix"], mesh.shape["chan"]),
        mesh=mesh, in_specs=placed, out_specs=P("pix", "chan", None), check_vma=False,
    )
```

```python
import functools

import jax
import jax.numpy as jnp
from jax import lax
from jax.experimental import pallas as pl
from jax.experimental.pallas import tpu as pltpu
from jax.sharding import PartitionSpec as P

MESH = pl.DeviceIdType.MESH
LANES = 128
TAPS = 7
HALO = 3
EDGE = 8
STRIP = 16
PARTS = 1
GROUP = 2


def kernel(
    n, m, x_ref, weight_ref, cbias_ref, gain_ref, shift_ref, ubias_ref, scale_ref, dbias_ref, up_hbm, down_hbm,
    out_ref,
    up, down, near, far, wide, residual, scales, biases, gath, normed, hidden,
    half_out, half_in, kept, cross_out, cross_in,
    up_sem, down_sem, near_send, near_recv, far_send, far_recv,
    gath_send, fwd_send, gath_recv, half_send, half_recv, cross_send, cross_recv,
):
    chunks, rows, width, _ = x_ref.shape
    span = width // PARTS
    pixels = rows * span
    chips = n // 2
    slots = n * chunks
    channels = slots * LANES
    block = channels // n
    sub = half_out.shape[1]
    steps = half_out.shape[0] // PARTS
    per_chip = steps // chips
    far_steps = steps - per_chip
    pix = lax.axis_index("pix")
    chan = lax.axis_index("chan")
    chip, core = pix // 2, pix % 2
    odd = chan % 2
    beside = chan + 1 - 2 * odd
    onward = chan + 2 - 4 * odd
    behind = chan - 2 + 4 * odd
    has_onward = (onward >= 0) & (onward < m)
    has_behind = (behind >= 0) & (behind < m)
    partner = pix + 1 - 2 * core

    def other(step):
        return ((chip + 1 + step) % chips) * 2 + core

    barrier = pltpu.get_barrier_semaphore()

    def greet(to_pix, to_chan):
        pl.semaphore_signal(
            barrier, inc=1, device_id={"pix": to_pix, "chan": to_chan}, device_id_type=MESH
        )

    greet(pix, beside)
    greet(partner, chan)
    for step in range(chips - 1):
        greet(other(step), chan)

    @pl.when(has_onward)
    def _():
        greet(pix, onward)

    @pl.when(has_behind)
    def _():
        greet(pix, behind)

    up_copy = pltpu.make_async_copy(up_hbm, up, up_sem)
    down_copy = pltpu.make_async_copy(down_hbm, down, down_sem)
    pl.semaphore_wait(
        barrier, 1 + chips + has_onward.astype(jnp.int32) + has_behind.astype(jnp.int32)
    )

    def remote(src, dst, send, recv, to_pix, to_chan):
        return pltpu.make_async_remote_copy(
            src_ref=src, dst_ref=dst, send_sem=send, recv_sem=recv,
            device_id={"pix": to_pix, "chan": to_chan}, device_id_type=MESH,
        )

    pieces = [(h, k) for h in range(PARTS) for k in range(chunks)]
    bounds = [0] + [span * (h + 1) + STRIP for h in range(PARTS - 1)] + [width]

    def fresh(h):
        return pl.ds(bounds[h], bounds[h + 1] - bounds[h])

    def near_copy(h, k):
        i = h * chunks + k
        return remote(
            x_ref.at[k, :, fresh(h)], near.at[k, :, fresh(h)], near_send.at[i], near_recv.at[i], pix, beside
        )

    def far_copy(h, k):
        i = h * chunks + k
        return remote(
            near.at[k, pl.ds(1 - odd, HALO), fresh(h)], far.at[k, :, fresh(h)],
            far_send.at[i], far_recv.at[i], pix, onward,
        )

    def own_copy(h, k, step):
        index = h * slots + pix * chunks + k
        to = partner if step == chips - 1 else other(step)
        return remote(
            gath.at[index], gath.at[index], gath_send.at[(step * PARTS + h) * chunks + k],
            gath_recv.at[index], to, chan,
        )

    def arrival(index):
        return remote(gath.at[index], gath.at[index], up_sem, gath_recv.at[index], partner, chan)

    def forward_copy(h, k, step):
        index = h * slots + other(step) * chunks + k
        return remote(
            gath.at[index], gath.at[index], fwd_send.at[(step * PARTS + h) * chunks + k],
            gath_recv.at[index], partner, chan,
        )

    for h, k in pieces:
        near_copy(h, k).start()
    up_copy.start()
    down_copy.start()

    wide[...] = jnp.zeros_like(wide)

    @pl.when(jnp.logical_not(has_behind))
    def _():
        far[...] = jnp.zeros_like(far)

    for k in range(chunks):
        for row in range(rows):
            residual[k * LANES : (k + 1) * LANES, row * width : (row + 1) * width] = (
                x_ref[k, row].astype(jnp.float32).T
            )
    for j in range(per_chip):
        lanes = slice(j * sub, (j + 1) * sub)
        scales[j] = jnp.broadcast_to(scale_ref[:, lanes], (width, sub)).T
        biases[j] = jnp.broadcast_to(dbias_ref[:, lanes], (width, sub)).T

    def pass_on(h, k):
        near_copy(h, k).wait_recv()

        @pl.when(has_onward)
        def _():
            far_copy(h, k).start()

    def filter_piece(h, k):
        @pl.when(has_behind)
        def _():
            far_copy(h, k).wait_recv()

        low = max(span * h - STRIP, 0)
        high = bounds[h + 1]
        inner = slice(EDGE + low, EDGE + high)
        some = slice(low, high)
        wide[HALO : HALO + rows, inner, :] = x_ref[k, :, some].astype(jnp.float32)
        wide[pl.ds((HALO + rows) * (1 - odd), HALO), inner, :] = near[
            k, pl.ds(odd * (rows - HALO), HALO), some
        ].astype(jnp.float32)
        wide[pl.ds((HALO + rows) * odd, HALO), inner, :] = far[k, :, some].astype(jnp.float32)
        bias = cbias_ref[k]
        own = h * slots + pix * chunks + k

        def strip(s, carry):
            place = pl.multiple_of(s * STRIP, STRIP)
            sums = [jnp.zeros((STRIP, LANES), jnp.float32) for _ in range(rows)]
            for b in range(TAPS):
                for i in range(rows + TAPS - 1):
                    piece = wide[i, pl.ds(place + (span * h + EDGE - HALO + b), STRIP), :]
                    for o in range(rows):
                        a = i - o
                        if 0 <= a < TAPS:
                            tap = a * TAPS + b
                            sums[o] = sums[o] + weight_ref[tap : tap + 1, k * LANES : (k + 1) * LANES] * piece
            for o in range(rows):
                gath[own, pl.ds(pl.multiple_of(o * span + place, STRIP), STRIP), :] = (
                    sums[o] + bias
                ).astype(jnp.bfloat16)
            return carry

        lax.fori_loop(0, span // STRIP, strip, 0)
        for step in range(chips):
            own_copy(h, k, step).start()

    def relay(h, k):
        for step in range(chips - 1):
            arrival(h * slots + other(step) * chunks + k).wait_recv()
            forward_copy(h, k, step).start()

    def settle(h):
        def one(k, carry):
            arrival(h * slots + partner * chunks + k).wait_recv()
            for step in range(chips - 1):
                mate = other(step) + 1 - 2 * core
                arrival(h * slots + mate * chunks + k).wait_recv()
            return carry

        lax.fori_loop(0, chunks, one, 0)

    count = len(pieces)
    early = chunks
    lag = 3
    for i in range(count + 1):
        if i < count:
            pass_on(*pieces[i])
        if i >= 1:
            filter_piece(*pieces[i - 1])
        if i >= lag and i - lag < early:
            relay(*pieces[i - lag])
    for i in range(max(count + 1 - lag, 0), early):
        relay(*pieces[i])

    band = 64

    def normalise(h):
        def one(s, carry):
            here = pl.ds(pl.multiple_of(s * band, band), band)
            first = jnp.zeros((band, LANES), jnp.float32)
            second = jnp.zeros((band, LANES), jnp.float32)
            for q in range(slots):
                v = gath[h * slots + q, here, :].astype(jnp.float32)
                first = first + v
                second = second + v * v
            mean = jnp.sum(first, axis=1, keepdims=True) / channels
            var = jnp.sum(second, axis=1, keepdims=True) / channels - mean * mean
            scale = lax.rsqrt(var + 1e-06)
            for q in range(slots):
                lanes = slice(q * LANES, (q + 1) * LANES)
                v = gath[h * slots + q, here, :].astype(jnp.float32)
                normed[here, lanes] = (
                    (v - mean) * scale * gain_ref[:, lanes] + shift_ref[:, lanes]
                ).astype(jnp.bfloat16)
            return carry

        lax.fori_loop(0, pixels // band, one, 0)

    units = up.shape[1]
    tile = 256
    pair = max(min(4, units // tile), 1)

    def gelu(v):
        return 0.5 * v * (1.0 + jnp.tanh(0.7978845608 * (v + 0.044715 * (v * v * v))))

    def expand(h):
        def one(s, carry):
            if h + 1 < PARTS:
                @pl.when(s < chunks)
                def _():
                    relay(h + 1, s)

            cols = [
                pl.ds(pl.multiple_of(s * (pair * tile), pair * tile) + u * tile, tile) for u in range(pair)
            ]
            sums = [
                jnp.dot(normed[...], up[:, c], preferred_element_type=jnp.float32) + ubias_ref[:, c]
                for c in cols
            ]
            for c, v in zip(cols, sums):
                hidden[:, c] = gelu(v).astype(jnp.bfloat16)
            return carry

        rounds = units // (pair * tile)
        lax.fori_loop(0, rounds, one, 0)
        if h + 1 < PARTS:
            for k in range(rounds, chunks):
                relay(h + 1, k)

    def half_copy(h, t):
        i = h * steps + t
        return remote(half_out.at[i], half_in.at[i], half_send.at[i], half_recv.at[i], partner, chan)

    def cross_copy(h, t):
        i = h * steps + t
        return remote(
            cross_out.at[i], cross_in.at[i], cross_send.at[i], cross_recv.at[i],
            other(t // per_chip), chan,
        )

    def contract(start):
        part = down[pl.ds(pl.multiple_of(start, sub), sub), :]
        return lax.dot_general(
            part, hidden[...], (((1,), (1,)), ((), ())), preferred_element_type=jnp.float32
        )

    def combine(h, t):
        half_copy(h, t).wait_recv()
        i = h * steps + t

        @pl.when(t < far_steps)
        def _():
            cross_out[i] = (kept[i] + half_in[i].astype(jnp.float32)).astype(jnp.bfloat16)
            cross_copy(h, t).start()

        @pl.when(t >= far_steps)
        def _():
            kept[i] = kept[i] + half_in[i].astype(jnp.float32)

    def reduce(h):
        def one(t, carry):
            @pl.when(t < steps)
            def _():
                owner = other(t // per_chip)
                away = owner + 1 - 2 * core
                row = (t % per_chip) * sub
                half_out[h * steps + t] = contract(away * block + row).astype(jnp.bfloat16)
                half_copy(h, t).start()

            @pl.when(t >= 1)
            def _():
                combine(h, t - 1)

            @pl.when(t < steps)
            def _():
                owner = other(t // per_chip)
                kept[h * steps + t] = contract(owner * block + (t % per_chip) * sub)

            return carry

        lax.fori_loop(0, steps + 1, one, 0)

    for h in range(PARTS):
        settle(h)
        normalise(h)
        if h == 0:
            up_copy.wait()
        expand(h)
        if h == 0:
            down_copy.wait()
        reduce(h)

    def finish(j, carry):
        totals = []
        for h in range(PARTS):
            total = kept[h * steps + far_steps + j]
            for step in range(chips - 1):
                t = step * per_chip + j
                cross_copy(h, t).wait_recv()
                total = total + cross_in[h * steps + t].astype(jnp.float32)
            totals.append(total)
        here = pl.ds(pl.multiple_of(j * sub, sub), sub)
        for r in range(rows):
            line = jnp.concatenate([total[:, r * span : (r + 1) * span] for total in totals], axis=1)
            columns = slice(r * width, (r + 1) * width)
            out_ref[here, columns] = (
                residual[here, columns] + scales[j] * (line + biases[j])
            ).astype(out_ref.dtype)
        return carry

    lax.fori_loop(0, per_chip, finish, 0)

    for h, k in pieces:
        near_copy(h, k).wait_send()
        for step in range(chips):
            own_copy(h, k, step).wait_send()
        for step in range(chips - 1):
            forward_copy(h, k, step).wait_send()

    @pl.when(has_onward)
    def _():
        for h, k in pieces:
            far_copy(h, k).wait_send()

    for h in range(PARTS):
        def sent(t, carry):
            half_copy(h, t).wait_send()

            @pl.when(t < far_steps)
            def _():
                cross_copy(h, t).wait_send()

            return carry

        lax.fori_loop(0, steps, sent, 0)


def on_device(
    n, m,
    images, conv_weight, conv_bias, norm_gain, norm_shift, up_weight, up_bias, down_weight, down_bias,
    layer_scale,
):
    chans, rows, width = images.shape
    pixels = rows * width
    chunks = chans // LANES
    channels, units = up_weight.shape
    chips = n // 2
    sub = min(GROUP * LANES, chans)
    steps = chips * (chans // sub)
    x = images.reshape(chunks, LANES, rows, width).transpose(0, 2, 3, 1)
    span = width // PARTS
    part = rows * span
    vmem = pl.BlockSpec(memory_space=pltpu.VMEM)
    hbm = pl.BlockSpec(memory_space=pl.ANY)
    bf16, f32 = jnp.bfloat16, jnp.float32
    dma = pltpu.SemaphoreType.DMA
    result = pl.pallas_call(
        functools.partial(kernel, n, m),
        out_shape=jax.ShapeDtypeStruct((chans, pixels), bf16),
        in_specs=[vmem] * 8 + [hbm] * 2,
        out_specs=vmem,
        scratch_shapes=[
            pltpu.VMEM((channels, units), bf16),
            pltpu.VMEM((channels, units), bf16),
            pltpu.VMEM((chunks, rows, width, LANES), bf16),
            pltpu.VMEM((chunks, HALO, width, LANES), bf16),
            pltpu.VMEM((rows + 2 * HALO, width + 2 * EDGE, LANES), f32),
            pltpu.VMEM((chans, pixels), f32),
            pltpu.VMEM((chans // sub, sub, width), f32),
            pltpu.VMEM((chans // sub, sub, width), f32),
            pltpu.VMEM((PARTS * n * chunks, part, LANES), bf16),
            pltpu.VMEM((part, channels), bf16),
            pltpu.VMEM((part, units), bf16),
            pltpu.VMEM((PARTS * steps, sub, part), bf16),
            pltpu.VMEM((PARTS * steps, sub, part), bf16),
            pltpu.VMEM((PARTS * steps, sub, part), f32),
            pltpu.VMEM((PARTS * steps, sub, part), bf16),
            pltpu.VMEM((PARTS * steps, sub, part), bf16),
            dma, dma,
            dma((PARTS * chunks,)), dma((PARTS * chunks,)), dma((PARTS * chunks,)), dma((PARTS * chunks,)),
            dma((PARTS * chips * chunks,)), dma((PARTS * chips * chunks,)), dma((PARTS * n * chunks,)),
            dma((PARTS * steps,)), dma((PARTS * steps,)), dma((PARTS * steps,)), dma((PARTS * steps,)),
        ],
        compiler_params=pltpu.CompilerParams(collective_id=0, has_side_effects=True),
    )(
        x, conv_weight.T, conv_bias.reshape(chunks, 1, LANES), norm_gain.reshape(1, channels),
        norm_shift.reshape(1, channels), up_bias.reshape(1, units), layer_scale.reshape(1, chans),
        down_bias.reshape(1, chans), up_weight, down_weight,
    )
    return result.reshape(chans, rows, width)


def solution(mesh):
    placed = (
        P("pix", "chan", None),
        P("pix", None),
        P("pix"),
        P(),
        P(),
        P(None, "pix"),
        P("pix"),
        P(None, "pix"),
        P("pix"),
        P("pix"),
    )
    return jax.shard_map(
        functools.partial(on_device, mesh.shape["pix"], mesh.shape["chan"]),
        mesh=mesh, in_specs=placed, out_specs=P("pix", "chan", None), check_vma=False,
    )
```
